1024 devices in a mesh: section: 8 (over y), dp: 32 (over z, core), tensor: 4 (over x).
Axes of the slice: x: 4, y: 8, z: 16, core: 2. Of those that a mesh axis runs over, the one named last changes fastest.
Arguments:
- out_grad: bfloat16 [4096, 4096], P('dp', 'tensor'), may hold values from -6 to 6
- section_out: bfloat16 [8, 4096, 4096], P('section', 'dp', 'tensor'), may hold values from -6 to 6
- context: bfloat16 [8, 4096, 2048], P('section', 'dp', 'tensor'), may hold values from -6 to 6
- queries: bfloat16 [8, 4096, 2048], P('section', 'dp', 'tensor')
- key_heads: bfloat16 [8, 4096, 2048], P('section', 'dp', 'tensor')
- values: bfloat16 [8, 4096, 2048], P('section', 'dp', 'tensor'), may hold values from -6 to 6
- o_weight: bfloat16 [8, 4096, 2048], P('section', None, 'tensor'), may hold values from -0.125 to 0.125
- doc_lengths: int32 [32], replicated, may hold values from 1 to 256, 4096 in all
Outputs:
- query_grad: bfloat16 [8, 4096, 2048], P('section', 'dp', 'tensor')
- key_grad: bfloat16 [8, 4096, 2048], P('section', 'dp', 'tensor')
- value_grad: bfloat16 [8, 4096, 2048], P('section', 'dp', 'tensor')
- o_weight_grad: float32 [8, 4096, 2048], P('section', 'dp', 'tensor')
The draws below stay inside these ranges and needn't reach their ends.
Inputs may be any that keep to these rules, and one draw needn't show every extreme that they name: `doc_lengths`: the lengths sum to 4096, and the longest document has exactly 256 patches.
All inputs are finite; a program needn't handle non-finite values.
Results may differ from the reference program's by a relative error of at most 0.023.
Values may be sent and summed in bfloat16 or wider, within the bound.
No kernel may reach another device: no remote copies, remote signals or barrier semaphores. Data moves between devices by JAX's collectives and lax.ppermute only.
A program may use at most 32 MiB of HBM per device.

```python
import math
import jax
import jax.numpy as jnp
import numpy as np
from jax import lax

D = 4096
HEADS = 16
HD = 128
ROWS = 128
REACH = 2
MOST = 256
DOCS = 32
SECTIONS = 8
ROWS_ALL = 4096
WIDE = 2048
N_DP = 32


def queries_and_keys(key):
    seeded = jax.random.fold_in(key, 4242)
    first, second = jax.random.split(seeded, 2)
    full_shape = (SECTIONS, ROWS_ALL, HEADS, HD)
    key_draw = jax.random.normal(first, full_shape, jnp.float32)
    query_draw = jax.random.normal(second, full_shape, jnp.float32)
    flat_shape = (SECTIONS, ROWS_ALL, HEADS * HD)
    return (query_draw.reshape(flat_shape), key_draw.reshape(flat_shape))


def draw_queries(key, part):
    return queries_and_keys(key)[0].astype(jnp.bfloat16)


def draw_key_heads(key, part):
    return queries_and_keys(key)[1].astype(jnp.bfloat16)


def raised(entries, own_key, source, target, shards_of, factor):
    owner, partner = [(jnp.arange(entries.shape[dim]) // (entries.shape[dim] // shards_of)).reshape([-1 if axis == dim else 1 for axis in range(entries.ndim)]) for dim in (source, target)]
    chosen = jax.random.permutation(own_key, shards_of)[partner]
    strong = (owner == chosen) | (owner == (partner + shards_of // 2) % shards_of)
    return jnp.where(strong, factor * entries, entries)


def shard_levels(key, dims, cuts, smallest, high):
    factor_of = 1.0
    for axis_at, blocks in cuts:
        draws = jax.random.uniform(jax.random.fold_in(jax.random.fold_in(key, 6), axis_at), (blocks,), jnp.float32, smallest / len(cuts), high / len(cuts))
        factor_of = factor_of * jnp.repeat(jnp.exp(draws), dims[axis_at] // blocks).reshape((-1,) + (1,) * (len(dims) - 1 - axis_at))
    return factor_of


def profile(number_of, total, limit, skew):
    portions = [(1 << 20) // math.isqrt(rank ** skew) + 1 for rank in range(2, number_of + 1)]
    rest, given = total - limit - (number_of - 1), [1] * (number_of - 1)
    while rest > 0:
        candidates = [i for i in range(number_of - 1) if given[i] < limit]
        whole, budget = sum([portions[i] for i in candidates]), rest
        for i in candidates:
            extra = min(limit - given[i], max(1, budget * portions[i] // whole), rest)
            given[i] = given[i] + extra
            rest = rest - extra
    return np.array([limit] + given)


def uneven_parts(key, number_of, total, limit, lean):
    if number_of == 2:
        one = jax.random.randint(key, (), max(1, total - limit), min(limit, total - 1) + 1)
        return jnp.stack([one, total - one])
    tallies = jnp.asarray(profile(number_of, total, limit, lean), jnp.int32)
    pairs = (number_of - 1) // 2
    donor, taker = tallies[1:1 + 2 * pairs:2], tallies[2:2 + 2 * pairs:2]
    margin = jnp.minimum(donor - 1, limit - taker)
    shifted = jax.random.randint(jax.random.fold_in(key, 1), (pairs,), 0, 1 << 20) % (margin + 1)
    tallies = tallies.at[1:1 + 2 * pairs:2].set(donor - shifted).at[2:2 + 2 * pairs:2].set(taker + shifted)
    return tallies[jax.random.permutation(jax.random.fold_in(key, 2), number_of)]


def noise(key, extent, spread, limit, shards=(), kind=jnp.bfloat16):
    level = shard_levels(key, extent, shards, -0.22, 0.18) if shards else 1.0
    result = jax.random.normal(key, extent, jnp.float32) * spread * level
    return jnp.minimum(jnp.maximum(result, -limit), limit).astype(kind)


def noise_with(own_key, shape, width, bound, cuts, heavy, kind=jnp.bfloat16):
    entries = width * jax.random.normal(own_key, shape, jnp.float32)
    if cuts:
        entries = entries * shard_levels(own_key, shape, cuts, -0.22, 0.18)
    return jnp.clip(raised(entries, jax.random.fold_in(own_key, 3), *heavy), -bound, bound).astype(kind)


def setup_inputs(seed: int = 0) -> dict:
    splits = jax.random.split(jax.random.key(seed), 9)
    out_grad = noise_with(splits[0], (ROWS_ALL, D), 1.0, 6.0, ((0, 32), (1, 4)), (0, 1, 32, 2.75))
    section_out = noise(splits[1], (SECTIONS, ROWS_ALL, D), 1.0, 6.0, ((0, 8), (1, 32), (2, 4)))
    context = noise(splits[2], (SECTIONS, ROWS_ALL, WIDE), 1.0, 6.0, ((0, 8), (1, 32), (2, 4)))
    queries = draw_queries(jax.random.fold_in(splits[8], 71), 0)
    key_heads = draw_key_heads(jax.random.fold_in(splits[8], 71), 0)
    values = noise(splits[5], (SECTIONS, ROWS_ALL, WIDE), 1.0, 6.0, ((0, 8), (1, 32), (2, 4)))
    o_weight = noise(splits[6], (SECTIONS, D, WIDE), WIDE ** -0.5, 0.125, ((0, 8), (2, 4)))
    doc_lengths = uneven_parts(splits[7], DOCS, ROWS_ALL, MOST, 2).astype(jnp.int32)
    return {"out_grad": out_grad, "section_out": section_out, "context": context, "queries": queries, "key_heads": key_heads, "values": values, "o_weight": o_weight, "doc_lengths": doc_lengths}


def rounded(value):
    return lax.optimization_barrier(value.astype(jnp.bfloat16))


def document_of(positions, ends):
    return jnp.sum((positions[:, None] >= ends[None, :]).astype(jnp.int32), axis=-1)


def one_section(out_grad, ends, inputs):
    upper, context, queries, key_heads, values, o_weight = inputs
    scaling = HD ** -0.5
    grad_rows = rounded(out_grad.astype(jnp.float32) + 0.25 * upper)
    d_context = rounded(jnp.dot(grad_rows, o_weight, preferred_element_type=jnp.float32))
    window = (REACH + 1) * ROWS
    front = REACH * ROWS
    three = (ROWS_ALL, HEADS, HD)
    padded_shape = (ROWS_ALL + front, HEADS, HD)
    dctx_f = d_context.astype(jnp.float32).reshape(three)
    ctx_f = context.astype(jnp.float32).reshape(three)
    query_f = queries.astype(jnp.float32).reshape(three)
    blank = jnp.zeros((front, WIDE), jnp.float32)
    key_pad = jnp.concatenate([blank, key_heads.astype(jnp.float32)], 0).reshape(padded_shape)
    value_pad = jnp.concatenate([blank, values.astype(jnp.float32)], 0).reshape(padded_shape)
    places = jnp.arange(ROWS, dtype=jnp.int32)
    spots = jnp.arange(window, dtype=jnp.int32)

    def block(carry, index):
        key_acc, value_acc = carry
        start = (index * ROWS).astype(jnp.int32)
        query_place = start + places
        key_place = start - front + spots
        allowed = (document_of(query_place, ends)[:, None] == document_of(key_place, ends)[None, :])
        allowed = allowed & (key_place[None, :] <= query_place[:, None]) & (key_place[None, :] >= 0)
        query_blk = lax.dynamic_slice_in_dim(query_f, start, ROWS, 0)
        dctx_blk = lax.dynamic_slice_in_dim(dctx_f, start, ROWS, 0)
        ctx_blk = lax.dynamic_slice_in_dim(ctx_f, start, ROWS, 0)
        key_win = lax.dynamic_slice_in_dim(key_pad, start, window, 0)
        value_win = lax.dynamic_slice_in_dim(value_pad, start, window, 0)
        scores = jnp.einsum("ihd,jhd->hij", query_blk, key_win) * scaling
        scores = jnp.where(allowed[None], scores, -jnp.inf)
        prob = jax.nn.softmax(scores, axis=-1)
        prob_b = rounded(prob).astype(jnp.float32)
        d_prob = jnp.einsum("ihd,jhd->hij", dctx_blk, value_win)
        delta = jnp.transpose(jnp.sum(dctx_blk * ctx_blk, axis=-1))
        d_score = rounded(prob * (d_prob - delta[..., None]) * scaling).astype(jnp.float32)
        query_out = jnp.einsum("hij,jhd->ihd", d_score, key_win).astype(jnp.bfloat16)
        key_part = jnp.einsum("hij,ihd->jhd", d_score, query_blk)
        value_part = jnp.einsum("hij,ihd->jhd", prob_b, dctx_blk)
        key_acc = lax.dynamic_update_slice_in_dim(key_acc, lax.dynamic_slice_in_dim(key_acc, start, window, 0) + key_part, start, 0)
        value_acc = lax.dynamic_update_slice_in_dim(value_acc, lax.dynamic_slice_in_dim(value_acc, start, window, 0) + value_part, start, 0)
        return (key_acc, value_acc), query_out

    zeros = jnp.zeros(padded_shape, jnp.float32)
    sums, query_blocks = lax.scan(block, (zeros, zeros), jnp.arange(N_DP, dtype=jnp.int32))
    query_grad = query_blocks.reshape(ROWS_ALL, WIDE)
    key_grad = sums[0][front:].reshape(ROWS_ALL, WIDE).astype(jnp.bfloat16)
    value_grad = sums[1][front:].reshape(ROWS_ALL, WIDE).astype(jnp.bfloat16)
    grad_blocks = grad_rows.reshape(N_DP, ROWS, D)
    ctx_blocks = context.reshape(N_DP, ROWS, WIDE)

    def add_block(index, total):
        grad_part = lax.dynamic_index_in_dim(grad_blocks, index, 0, keepdims=False)
        ctx_part = lax.dynamic_index_in_dim(ctx_blocks, index, 0, keepdims=False)
        term = jnp.dot(grad_part.T, ctx_part, preferred_element_type=jnp.float32)
        return total + rounded(term).astype(jnp.float32)

    weight_grad = lax.fori_loop(0, N_DP, add_block, jnp.zeros((D, WIDE), jnp.float32))
    return (query_grad, key_grad, value_grad, weight_grad)


def reference(out_grad, section_out, context, queries, key_heads, values, o_weight, doc_lengths):
    section_f = section_out.astype(jnp.float32)
    upper = jnp.flip(jnp.cumsum(jnp.flip(section_f, 0), axis=0), 0)
    ends = jnp.cumsum(doc_lengths).astype(jnp.int32)
    results = lax.map(lambda inputs: one_section(out_grad, ends, inputs), (upper, context, queries, key_heads, values, o_weight))
    return (results[0], results[1], results[2], results[3])
```

```python
import functools

import jax
import jax.numpy as jnp
from jax import lax
from jax.experimental import pallas as pl
from jax.experimental.pallas import tpu as pltpu
from jax.sharding import Mesh, PartitionSpec as P

HD = 128
REACH = 2
CORES = 2
F32 = jnp.float32
BF16 = jnp.bfloat16
WHOLE = pl.BlockSpec(memory_space=pltpu.VMEM)
SCALARS = pl.BlockSpec(memory_space=pltpu.SMEM)
DP = ("z", "core")


def contract(a, b, left, right):
    return lax.dot_general(
        a, b, (((left,), (right,)), ((), ())), preferred_element_type=F32
    )


def shifted(value, steps):
    count = lax.axis_size("z") * lax.axis_size("core")
    return lax.ppermute(value, DP, [(i, (i + steps) % count) for i in range(count)])


def exchanged(value, axis):
    return lax.all_to_all(value, axis, 0, 0, tiled=True)


def spread(value, axis):
    copies = lax.axis_size(axis)
    return exchanged(jnp.broadcast_to(value[None], (copies, *value.shape)), axis)


def suffix_kernel(out_grad_ref, layers_ref, grads_ref):
    count, rows, _ = layers_ref.shape
    at = pl.multiple_of(lax.axis_index("section") * rows, rows)
    base = out_grad_ref[pl.ds(at, rows), :].astype(F32)
    upper = None
    for layer in range(count - 1, -1, -1):
        own = layers_ref[layer].astype(F32)
        upper = own if upper is None else upper + own
        grads_ref[layer] = (base + 0.25 * upper).astype(BF16)


def prob_kernel(lengths_ref, query_ref, own_ref, near_ref, far_ref, prob_ref):
    rows, width = query_ref.shape
    window = (REACH + 1) * rows
    block = lax.axis_index("z") * CORES + lax.axis_index("core")
    first = block * rows
    place = first + lax.broadcasted_iota(jnp.int32, (rows, window), 0)
    keys = first - REACH * rows + lax.broadcasted_iota(jnp.int32, (rows, window), 1)
    narrow = first + lax.broadcasted_iota(jnp.int32, (rows, HD), 0)

    def advance(k, carry):
        end, start = carry
        end = end + lengths_ref[k]
        return end, jnp.where(narrow >= end, end, start)

    start = lax.fori_loop(
        0, lengths_ref.shape[0], advance, (jnp.int32(0), jnp.zeros((rows, HD), jnp.int32))
    )[1]
    start = jnp.concatenate([start] * (window // HD), axis=1)
    allowed = (keys <= place) & (keys >= start)
    for head in range(width // HD):
        cols = slice(head * HD, (head + 1) * HD)
        query = query_ref[:, cols]
        scores = jnp.concatenate(
            [contract(query, ref[0, :, cols], 1, 1) for ref in (far_ref, near_ref, own_ref)],
            axis=1,
        )
        scores = jnp.where(allowed, scores * HD ** (-0.5), -jnp.inf)
        top = jnp.max(scores, axis=-1, keepdims=True)
        weight = jnp.exp(scores - top)
        prob_ref[head] = weight / jnp.sum(weight, axis=-1, keepdims=True)


def grads_kernel(
    grad_ref, weight_ref, prob_ref, query_ref, own_ref, near_ref, far_ref, context_ref,
    query_grad_ref, own_part_ref, near_part_ref, far_part_ref,
):
    parts, rows, width = grad_ref.shape
    total = None
    for part in range(parts):
        term = jnp.dot(
            grad_ref[part],
            weight_ref[part * width : (part + 1) * width, :],
            preferred_element_type=F32,
        )
        total = term if total is None else total + term
    d_context = total.astype(BF16)
    blocks = ((far_ref, far_part_ref), (near_ref, near_part_ref), (own_ref, own_part_ref))
    for head in range(query_ref.shape[1] // HD):
        cols = slice(head * HD, (head + 1) * HD)
        query = query_ref[:, cols]
        dctx = d_context[:, cols]
        delta = jnp.sum(
            dctx.astype(F32) * context_ref[:, cols].astype(F32), axis=-1, keepdims=True
        )
        query_grad = None
        for index, (held, part_ref) in enumerate(blocks):
            prob = prob_ref[head, :, index * rows : (index + 1) * rows]
            d_prob = contract(dctx, held[1, :, cols], 1, 1)
            d_score = (prob * (d_prob - delta) * HD ** (-0.5)).astype(BF16)
            term = jnp.dot(d_score, held[0, :, cols], preferred_element_type=F32)
            query_grad = term if query_grad is None else query_grad + term
            part_ref[0, :, cols] = contract(d_score, query, 0, 0).astype(part_ref.dtype)
            part_ref[1, :, cols] = contract(prob.astype(BF16), dctx, 0, 0).astype(part_ref.dtype)
        query_grad_ref[:, cols] = query_grad.astype(BF16)


def weight_kernel(grad_ref, context_ref, keep_ref, send_ref):
    quarters, blocks, rows, features = grad_ref.shape
    total = None
    for quarter in range(quarters):
        grad = grad_ref[quarter].reshape(blocks * rows, features)
        context = context_ref[:, quarter * rows : (quarter + 1) * rows, :]
        term = contract(grad, context.reshape(blocks * rows, context.shape[-1]), 0, 0)
        total = term if total is None else total + term
    half = features // CORES
    first, second = total[:half], total[half:]
    is_first = lax.axis_index("core") == 0
    keep_ref[...] = jnp.where(is_first, first, second)
    send_ref[...] = jnp.where(is_first, second, first).astype(BF16)


def call(kernel, outs, inputs, specs, flops, nbytes):
    return pl.pallas_call(
        kernel,
        out_shape=outs,
        in_specs=specs,
        out_specs=[WHOLE] * len(outs),
        cost_estimate=pl.CostEstimate(flops=flops, bytes_accessed=nbytes, transcendentals=0),
        compiler_params=pltpu.CompilerParams(vmem_limit_bytes=28 * 2**20),
    )(*inputs)


def on_device(out_grad, section_out, context, queries, key_heads, values, o_weight, doc_lengths):
    rows, width = queries.shape[1:]
    features = out_grad.shape[1]
    sections, tensors, chips = (lax.axis_size(a) for a in ("section", "tensor", "z"))
    heads = width // HD
    window = (REACH + 1) * rows
    shape = jax.ShapeDtypeStruct

    context_all = lax.all_gather(context[0], "z")

    layers = exchanged(section_out.reshape(sections, rows // sections, features), "section")
    held = jnp.concatenate([key_heads, values], 0)
    near = shifted(held, 1)
    far = shifted(held, 2)
    (grads,) = call(
        suffix_kernel,
        [shape(layers.shape, BF16)],
        (out_grad, layers),
        [WHOLE] * 2,
        layers.size * 3,
        layers.size * 4,
    )
    grad_local = exchanged(grads, "section").reshape(rows, features)
    (prob,) = call(
        prob_kernel,
        [shape((heads, rows, window), F32)],
        (doc_lengths, queries[0], held, near, far),
        [SCALARS] + [WHOLE] * 4,
        heads * rows * window * (2 * HD + 10),
        heads * rows * window * 8,
    )
    grad_full = spread(grad_local, "tensor")

    quarter = rows // tensors
    mine = lax.dynamic_slice_in_dim(grad_full, lax.axis_index("tensor") * quarter, quarter, 1)
    pieces = chips // tensors
    mine = jnp.transpose(
        mine.reshape(tensors, quarter, pieces, features // pieces), (0, 2, 1, 3)
    ).reshape(chips, quarter, features // pieces)
    columns = exchanged(mine, "z")

    query_grad, own_part, near_part, far_part = call(
        grads_kernel,
        [
            shape((rows, width), BF16),
            shape((2, rows, width), F32),
            shape((2, rows, width), BF16),
            shape((2, rows, width), BF16),
        ],
        (grad_full, o_weight[0], prob, queries[0], held, near, far, context[0]),
        [WHOLE] * 8,
        2 * rows * features * tensors * width + 8 * rows * window * width,
        2 * features * tensors * width,
    )
    near_back = shifted(near_part, -1)
    far_back = shifted(far_part, -2)
    sums = (own_part + near_back.astype(F32) + far_back.astype(F32)).astype(BF16)

    columns_all = spread(columns, "tensor")
    keep, send = call(
        weight_kernel,
        [shape((rows, width), F32), shape((rows, width), BF16)],
        (columns_all, context_all),
        [WHOLE] * 2,
        2 * columns_all.size * width,
        2 * (columns_all.size + context_all.size),
    )
    other = lax.ppermute(send, "core", [(i, CORES - 1 - i) for i in range(CORES)])
    weight_grad = keep + other.astype(F32)
    return query_grad[None], sums[:1], sums[1:], weight_grad[None]


def solution(mesh):
    sections, shards, tensors = mesh.devices.shape
    split = Mesh(
        mesh.devices.reshape(sections, shards // CORES, CORES, tensors),
        ("section", "z", "core", "tensor"),
    )
    placed = P("section", DP, "tensor")
    return jax.shard_map(
        on_device,
        mesh=split,
        in_specs=(
            P(DP, "tensor"), placed, placed, placed, placed, placed,
            P("section", None, "tensor"), P(),
        ),
        out_specs=(placed,) * 4,
        check_vma=False,
    )
```

```python
import jax
import jax.numpy as jnp
from jax import lax
from jax.experimental import pallas as pl
from jax.experimental.pallas import tpu as pltpu
from jax.sharding import Mesh, PartitionSpec as P


HD = 128
REACH = 2
CORES = 2
NEAR = 2
F32 = jnp.float32
BF16 = jnp.bfloat16
WHOLE = pl.BlockSpec(memory_space=pltpu.VMEM)
SCALARS = pl.BlockSpec(memory_space=pltpu.SMEM)
DP = ("zh", "zl", "core")
GROUP = ("zl", "core")


def contract(a, b, left, right):
    return lax.dot_general(
        a, b, (((left,), (right,)), ((), ())), preferred_element_type=F32
    )


def shifted(value, steps):
    count = lax.axis_size(DP)
    return lax.ppermute(value, DP, [(i, (i + steps) % count) for i in range(count)])


def turned(value, steps):
    count = lax.axis_size("tensor")
    return lax.ppermute(value, "tensor", [(i, (i + steps) % count) for i in range(count)])


def exchanged(value, axis):
    return lax.all_to_all(value, axis, 0, 0, tiled=True)


def spread(value, axis):
    copies = lax.axis_size(axis)
    return exchanged(jnp.broadcast_to(value[None], (copies, *value.shape)), axis)


def slice_kernel(own_ref, sliced_ref):
    lanes = sliced_ref.shape[-1]
    for at in range(sliced_ref.shape[0]):
        sliced_ref[at] = own_ref[:, at * lanes : (at + 1) * lanes]


def suffix_kernel(out_grad_ref, layers_ref, grads_ref):
    count, _, lanes = layers_ref.shape
    quarters, _, rows, _ = grads_ref.shape
    at = pl.multiple_of(lax.axis_index("section") * lanes, lanes)
    base = out_grad_ref[:, pl.ds(at, lanes)].astype(F32)
    upper = None
    for layer in range(count - 1, -1, -1):
        own = layers_ref[layer].astype(F32)
        upper = own if upper is None else upper + own
        grads = (base + 0.25 * upper).astype(BF16)
        for quarter in range(quarters):
            grads_ref[quarter, layer] = grads[quarter * rows : (quarter + 1) * rows]


def prob_kernel(lengths_ref, query_ref, own_ref, near_ref, far_ref, prob_ref):
    rows, width = query_ref.shape
    window = (REACH + 1) * rows
    block = lax.axis_index(DP)
    first = block * rows
    place = first + lax.broadcasted_iota(jnp.int32, (rows, window), 0)
    keys = first - REACH * rows + lax.broadcasted_iota(jnp.int32, (rows, window), 1)
    narrow = first + lax.broadcasted_iota(jnp.int32, (rows, HD), 0)

    def advance(k, carry):
        end, start = carry
        end = end + lengths_ref[k]
        return end, jnp.where(narrow >= end, end, start)

    start = lax.fori_loop(
        0, lengths_ref.shape[0], advance, (jnp.int32(0), jnp.zeros((rows, HD), jnp.int32))
    )[1]
    start = jnp.concatenate([start] * (window // HD), axis=1)
    allowed = (keys <= place) & (keys >= start)
    for head in range(width // HD):
        cols = slice(head * HD, (head + 1) * HD)
        query = query_ref[:, cols]
        scores = jnp.concatenate(
            [contract(query, ref[0, :, cols], 1, 1) for ref in (far_ref, near_ref, own_ref)],
            axis=1,
        )
        scores = jnp.where(allowed, scores * HD ** (-0.5), -jnp.inf)
        top = jnp.max(scores, axis=-1, keepdims=True)
        weight = jnp.exp(scores - top)
        prob_ref[head] = weight / jnp.sum(weight, axis=-1, keepdims=True)


def grads_kernel(
    mine_ref, left_ref, right_ref, first_ref, second_ref,
    weight_ref, prob_ref, query_ref, own_ref, near_ref, far_ref, context_ref,
    query_grad_ref, own_part_ref, near_part_ref, far_part_ref, d_context_ref,
):
    quarter = mine_ref.shape[1]
    rows = query_ref.shape[0]
    count = rows // quarter
    held_rows = (
        (0, (mine_ref,)), (1, (right_ref,)), (count - 1, (left_ref,)),
        (2, (first_ref, second_ref)),
    )[: min(count, 4)]
    grad = jnp.concatenate(
        [
            jnp.concatenate([ref[at] for ref in refs for at in range(ref.shape[0])], axis=1)
            for _, refs in held_rows
        ],
        axis=0,
    )
    total = jnp.dot(grad, weight_ref[...], preferred_element_type=F32).astype(BF16)
    for index, (steps, _) in enumerate(held_rows):
        at = lax.rem(lax.axis_index("tensor") + steps, count) * quarter
        d_context_ref[pl.ds(pl.multiple_of(at, quarter), quarter), :] = total[
            index * quarter : (index + 1) * quarter
        ]
    d_context = d_context_ref[...]
    blocks = ((far_ref, far_part_ref), (near_ref, near_part_ref), (own_ref, own_part_ref))
    for head in range(query_ref.shape[1] // HD):
        cols = slice(head * HD, (head + 1) * HD)
        query = query_ref[:, cols]
        dctx = d_context[:, cols]
        delta = jnp.sum(
            dctx.astype(F32) * context_ref[:, cols].astype(F32), axis=-1, keepdims=True
        )
        query_grad = None
        for index, (held, part_ref) in enumerate(blocks):
            prob = prob_ref[head, :, index * rows : (index + 1) * rows]
            d_prob = contract(dctx, held[1, :, cols], 1, 1)
            d_score = (prob * (d_prob - delta) * HD ** (-0.5)).astype(BF16)
            term = jnp.dot(d_score, held[0, :, cols], preferred_element_type=F32)
            query_grad = term if query_grad is None else query_grad + term
            part_ref[0, :, cols] = contract(d_score, query, 0, 0).astype(part_ref.dtype)
            part_ref[1, :, cols] = contract(prob.astype(BF16), dctx, 0, 0).astype(part_ref.dtype)
        query_grad_ref[:, cols] = query_grad.astype(BF16)


def weight_kernel(grad_ref, context_ref, terms_ref):
    quarters, blocks, owners, rows, lanes = grad_ref.shape
    for owner in range(owners):
        total = None
        for quarter in range(quarters):
            grad = grad_ref[quarter, :, owner].reshape(blocks * rows, lanes)
            context = context_ref[:, quarter * rows : (quarter + 1) * rows, :]
            term = contract(grad, context.reshape(blocks * rows, context.shape[-1]), 0, 0)
            total = term if total is None else total + term
        terms_ref[owner] = total.astype(BF16)


def call(kernel, outs, inputs, specs, flops, nbytes, scratch=()):
    return pl.pallas_call(
        kernel,
        out_shape=outs,
        in_specs=specs,
        out_specs=[WHOLE] * len(outs),
        scratch_shapes=list(scratch),
        cost_estimate=pl.CostEstimate(flops=flops, bytes_accessed=nbytes, transcendentals=0),
        compiler_params=pltpu.CompilerParams(vmem_limit_bytes=28 * 2**20),
    )(*inputs)


def on_device(out_grad, section_out, context, queries, key_heads, values, o_weight, doc_lengths):
    rows, width = queries.shape[1:]
    features = out_grad.shape[1]
    sections, tensors, chips = (lax.axis_size(a) for a in ("section", "tensor", "zh"))
    owners = lax.axis_size(GROUP)
    heads = width // HD
    window = (REACH + 1) * rows
    lanes = features // sections
    quarter = rows // tensors
    pieces = sections * tensors
    shape = jax.ShapeDtypeStruct

    context_all = lax.all_gather(context[0], "zh")

    (sliced,) = call(
        slice_kernel,
        [shape((sections, rows, lanes), BF16)],
        (section_out[0],),
        [WHOLE],
        0,
        4 * rows * features,
    )
    layers = exchanged(sliced, "section")
    held = jnp.concatenate([key_heads, values], 0)
    near = shifted(held, 1)
    far = shifted(held, 2)
    (grads,) = call(
        suffix_kernel,
        [shape((tensors, sections, quarter, lanes), BF16)],
        (out_grad, layers),
        [WHOLE] * 2,
        layers.size * 3,
        layers.size * 4,
    )
    (prob,) = call(
        prob_kernel,
        [shape((heads, rows, window), F32)],
        (doc_lengths, queries[0], held, near, far),
        [SCALARS] + [WHOLE] * 4,
        heads * rows * window * (2 * HD + 10),
        heads * rows * window * 8,
    )
    mine = exchanged(grads.reshape(pieces, quarter, lanes), ("tensor", "section"))
    columns = exchanged(mine.reshape(chips, owners, quarter, lanes), "zh")
    half = pieces // 2
    from_left = turned(mine, 1)
    from_right = turned(mine, -1)
    far_first = turned(from_left[:half], 1)
    far_second = turned(from_right[half:], -1)
    columns_all = spread(columns, "tensor")

    query_grad, own_part, near_part, far_part = call(
        grads_kernel,
        [
            shape((rows, width), BF16),
            shape((2, rows, width), F32),
            shape((2, rows, width), BF16),
            shape((2, rows, width), BF16),
        ],
        (
            mine, from_left, from_right, far_first, far_second,
            o_weight[0], prob, queries[0], held, near, far, context[0],
        ),
        [WHOLE] * 12,
        2 * rows * features * tensors * width + 8 * rows * window * width,
        2 * features * tensors * width,
        [pltpu.VMEM((rows, width), BF16)],
    )
    near_back = shifted(near_part, -1)
    far_back = shifted(far_part, -2)
    sums = (own_part + near_back.astype(F32) + far_back.astype(F32)).astype(BF16)

    (terms,) = call(
        weight_kernel,
        [shape((owners, lanes, width), BF16)],
        (columns_all, context_all),
        [WHOLE] * 2,
        2 * columns_all.size * width,
        2 * (columns_all.size + context_all.size),
    )
    gathered = exchanged(terms, GROUP)
    weight_grad = jnp.sum(gathered.astype(F32), axis=0)
    return query_grad[None], sums[:1], sums[1:], weight_grad[None]


def solution(mesh):
    sections, shards, tensors = mesh.devices.shape
    split = Mesh(
        mesh.devices.reshape(sections, shards // (CORES * NEAR), NEAR, CORES, tensors),
        ("section", *DP, "tensor"),
    )
    placed = P("section", DP, "tensor")

    return jax.shard_map(
        on_device,
        mesh=split,
        in_specs=(
            P(DP, "tensor"), placed, placed, placed, placed, placed,
            P("section", None, "tensor"), P(),
        ),
        out_specs=(placed,) * 4,
        check_vma=False,
    )
```

```python
import jax
import jax.numpy as jnp
from jax import lax
from jax.experimental import pallas as pl
from jax.experimental.pallas import tpu as pltpu
from jax.sharding import Mesh, PartitionSpec as P


HD = 128
REACH = 2
CORES = 2
NEAR = 2
F32 = jnp.float32
BF16 = jnp.bfloat16
WHOLE = pl.BlockSpec(memory_space=pltpu.VMEM)
RAW = pl.BlockSpec(memory_space=pltpu.HBM)
DP = ("zh", "zl", "core")
GROUP = ("zl", "core")


def contract(a, b, left, right):
    return lax.dot_general(
        a, b, (((left,), (right,)), ((), ())), preferred_element_type=F32
    )


def shifted(value, steps):
    count = lax.axis_size(DP)
    return lax.ppermute(value, DP, [(i, (i + steps) % count) for i in range(count)])


def turned(value, axis, steps):
    count = lax.axis_size(axis)
    return lax.ppermute(value, axis, [(i, (i + steps) % count) for i in range(count)])


def swapped(value, mask):
    count = lax.axis_size(GROUP)
    return lax.ppermute(value, GROUP, [(i, i ^ mask) for i in range(count)])


def exchanged(value, axis):
    return lax.all_to_all(value, axis, 0, 0, tiled=True)


def spread(value, axis):
    copies = lax.axis_size(axis)
    return exchanged(jnp.broadcast_to(value[None], (copies, *value.shape)), axis)


def copy_all(copies):
    for copy in copies:
        copy.start()
    for copy in copies:
        copy.wait()


def slice_kernel(own_ref, sliced_ref, sems):
    count, _, lanes = sliced_ref.shape
    copy_all(
        [
            pltpu.make_async_copy(
                own_ref.at[:, pl.ds(at * lanes, lanes)], sliced_ref.at[at], sems.at[at]
            )
            for at in range(count)
        ]
    )


def pack_kernel(keys_ref, values_ref, out_grad_ref, held_ref, base_ref, sems):
    lanes = base_ref.shape[1]
    at = pl.multiple_of(lax.axis_index("section") * lanes, lanes)
    copy_all(
        [
            pltpu.make_async_copy(keys_ref.at[0], held_ref.at[0], sems.at[0]),
            pltpu.make_async_copy(values_ref.at[0], held_ref.at[1], sems.at[1]),
            pltpu.make_async_copy(out_grad_ref.at[:, pl.ds(at, lanes)], base_ref, sems.at[2]),
        ]
    )


def suffix_kernel(base_ref, layers_ref, grads_ref):
    count = layers_ref.shape[0]
    quarters, _, rows, _ = grads_ref.shape
    base = base_ref[...].astype(F32)
    upper = None
    for layer in range(count - 1, -1, -1):
        own = layers_ref[layer].astype(F32)
        upper = own if upper is None else upper + own
        grads = (base + 0.25 * upper).astype(BF16)
        for quarter in range(quarters):
            grads_ref[quarter, layer] = grads[quarter * rows : (quarter + 1) * rows]


def prob_kernel(
    lengths_hbm, query_hbm, own_ref, near_ref, far_ref,
    prob_ref, lengths_ref, query_ref, sems,
):
    lengths_copy = pltpu.make_async_copy(lengths_hbm, lengths_ref, sems.at[0])
    query_copy = pltpu.make_async_copy(query_hbm.at[0], query_ref, sems.at[1])
    lengths_copy.start()
    query_copy.start()
    rows, width = query_ref.shape
    window = (REACH + 1) * rows
    block = lax.axis_index(DP)
    first = block * rows
    place = first + lax.broadcasted_iota(jnp.int32, (rows, window), 0)
    keys = first - REACH * rows + lax.broadcasted_iota(jnp.int32, (rows, window), 1)
    narrow = first + lax.broadcasted_iota(jnp.int32, (rows, HD), 0)

    def advance(k, carry):
        end, start = carry
        end = end + lengths_ref[k]
        return end, jnp.where(narrow >= end, end, start)

    lengths_copy.wait()
    start = lax.fori_loop(
        0, lengths_ref.shape[0], advance, (jnp.int32(0), jnp.zeros((rows, HD), jnp.int32))
    )[1]
    start = jnp.concatenate([start] * (window // HD), axis=1)
    allowed = (keys <= place) & (keys >= start)
    query_copy.wait()
    for head in range(width // HD):
        cols = slice(head * HD, (head + 1) * HD)
        query = query_ref[:, cols]
        scores = jnp.concatenate(
            [contract(query, ref[0, :, cols], 1, 1) for ref in (far_ref, near_ref, own_ref)],
            axis=1,
        )
        scores = jnp.where(allowed, scores * HD ** (-0.5), -jnp.inf)
        top = jnp.max(scores, axis=-1, keepdims=True)
        weight = jnp.exp(scores - top)
        prob_ref[head] = weight / jnp.sum(weight, axis=-1, keepdims=True)


def grads_kernel(
    mine_ref, left_ref, right_ref, across_ref,
    weight_hbm, prob_ref, query_ref, own_ref, near_ref, far_ref, context_ref,
    query_grad_ref, own_part_ref, near_part_ref, far_part_ref,
    d_context_ref, weight_ref, sems,
):
    pieces, quarter, lanes = mine_ref.shape
    rows = query_ref.shape[0]
    count = rows // quarter
    held_rows = ((0, mine_ref), (1, right_ref), (count - 1, left_ref), (2, across_ref))[:count]
    chunks = sems.shape[0]
    step = pieces // chunks
    depth = step * lanes
    copies = [
        pltpu.make_async_copy(
            weight_hbm.at[0, pl.ds(chunk * depth, depth)],
            weight_ref.at[pl.ds(chunk * depth, depth)],
            sems.at[chunk],
        )
        for chunk in range(chunks)
    ]
    for copy in copies:
        copy.start()
    total = None
    for chunk in range(chunks):
        grad = jnp.concatenate(
            [
                jnp.concatenate(
                    [ref[at] for at in range(chunk * step, (chunk + 1) * step)], axis=1
                )
                for _, ref in held_rows
            ],
            axis=0,
        )
        copies[chunk].wait()
        term = jnp.dot(
            grad, weight_ref[chunk * depth : (chunk + 1) * depth, :], preferred_element_type=F32
        )
        total = term if total is None else total + term
    total = total.astype(BF16)
    for index, (steps, _) in enumerate(held_rows):
        at = lax.rem(lax.axis_index("tensor") + steps, count) * quarter
        d_context_ref[pl.ds(pl.multiple_of(at, quarter), quarter), :] = total[
            index * quarter : (index + 1) * quarter
        ]
    d_context = d_context_ref[...]
    blocks = ((far_ref, far_part_ref), (near_ref, near_part_ref), (own_ref, own_part_ref))
    for head in range(query_ref.shape[1] // HD):
        cols = slice(head * HD, (head + 1) * HD)
        query = query_ref[:, cols]
        dctx = d_context[:, cols]
        delta = jnp.sum(
            dctx.astype(F32) * context_ref[:, cols].astype(F32), axis=-1, keepdims=True
        )
        query_grad = None
        for index, (held, part_ref) in enumerate(blocks):
            prob = prob_ref[head, :, index * rows : (index + 1) * rows]
            d_prob = contract(dctx, held[1, :, cols], 1, 1)
            d_score = (prob * (d_prob - delta) * HD ** (-0.5)).astype(BF16)
            term = jnp.dot(d_score, held[0, :, cols], preferred_element_type=F32)
            query_grad = term if query_grad is None else query_grad + term
            part_ref[0, :, cols] = contract(d_score, query, 0, 0).astype(part_ref.dtype)
            part_ref[1, :, cols] = contract(prob.astype(BF16), dctx, 0, 0).astype(part_ref.dtype)
        query_grad_ref[:, cols] = query_grad.astype(BF16)


def weight_kernel(grad_ref, *refs):
    quarters, blocks, owners, rows, _ = grad_ref.shape
    context_refs, term_refs = refs[:blocks], refs[blocks:]
    here, me = lax.axis_index("zh"), lax.axis_index(GROUP)
    places = [lax.rem(here + steps, blocks) for steps in ring_steps(blocks)]
    contexts = [
        jnp.concatenate([ref[quarter * rows : (quarter + 1) * rows] for ref in context_refs], axis=0)
        for quarter in range(quarters)
    ]
    for mask in range(owners):
        owner = jnp.bitwise_xor(me, mask)
        total = None
        for quarter in range(quarters):
            grad = jnp.concatenate([grad_ref[quarter, at, owner] for at in places], axis=0)
            term = contract(grad, contexts[quarter], 0, 0)
            total = term if total is None else total + term
        term_refs[mask][...] = total.astype(term_refs[mask].dtype)


def ring_steps(count):
    steps = [0]
    for hop in range(1, count // 2 + 1):
        steps.append(count - hop)
        if hop < count - hop:
            steps.append(hop)
    return steps


def call(kernel, outs, inputs, specs, flops, nbytes, scratch=()):
    return pl.pallas_call(
        kernel,
        out_shape=outs,
        in_specs=specs,
        out_specs=[WHOLE] * len(outs),
        scratch_shapes=list(scratch),
        compiler_params=pltpu.CompilerParams(vmem_limit_bytes=24 * 2**20),
        cost_estimate=pl.CostEstimate(flops=flops, bytes_accessed=nbytes, transcendentals=0),
    )(
        *(
            pltpu.with_memory_space_constraint(value, pltpu.HBM) if spec is RAW else value
            for value, spec in zip(inputs, specs)
        )
    )


def on_device(out_grad, section_out, context, queries, key_heads, values, o_weight, doc_lengths):
    rows, width = queries.shape[1:]
    features = out_grad.shape[1]
    sections, tensors, chips = (lax.axis_size(a) for a in ("section", "tensor", "zh"))
    owners = lax.axis_size(GROUP)
    heads = width // HD
    window = (REACH + 1) * rows
    lanes = features // sections
    quarter = rows // tensors
    pieces = sections * tensors
    shape = jax.ShapeDtypeStruct

    (sliced,) = call(
        slice_kernel,
        [shape((sections, rows, lanes), BF16)],
        (section_out[0],),
        [RAW],
        0,
        4 * rows * features,
        [pltpu.SemaphoreType.DMA((sections,))],
    )
    layers = exchanged(sliced, "section")
    held, base = call(
        pack_kernel,
        [shape((2, rows, width), BF16), shape((rows, lanes), BF16)],
        (key_heads, values, out_grad),
        [RAW] * 3,
        0,
        8 * rows * width,
        [pltpu.SemaphoreType.DMA((3,))],
    )
    blocks = [context[0]]
    for hop in range(1, chips // 2 + 1):
        blocks.append(turned(blocks[max(len(blocks) - 2, 0)], "zh", 1))
        if hop < chips - hop:
            blocks.append(turned(blocks[max(len(blocks) - 2, 0)], "zh", -1))
    near = shifted(held, 1)
    far = shifted(held, 2)
    (grads,) = call(
        suffix_kernel,
        [shape((tensors, sections, quarter, lanes), BF16)],
        (base, layers),
        [WHOLE] * 2,
        layers.size * 3,
        layers.size * 4,
    )
    mine = exchanged(grads.reshape(pieces, quarter, lanes), ("tensor", "section"))
    (prob,) = call(
        prob_kernel,
        [shape((heads, rows, window), F32)],
        (doc_lengths, queries, held, near, far),
        [RAW] * 2 + [WHOLE] * 3,
        heads * rows * window * (2 * HD + 10),
        heads * rows * window * 8,
        [
            pltpu.SMEM(doc_lengths.shape, jnp.int32),
            pltpu.VMEM((rows, width), BF16),
            pltpu.SemaphoreType.DMA((2,)),
        ],
    )
    columns = exchanged(mine.reshape(chips, owners, quarter, lanes), "zh")
    from_left = turned(mine, "tensor", 1)
    from_right = turned(mine, "tensor", -1)
    across = turned(from_left, "tensor", 1)
    columns_all = spread(columns, "tensor")

    query_grad, own_part, near_part, far_part = call(
        grads_kernel,
        [
            shape((rows, width), BF16),
            shape((2, rows, width), F32),
            shape((2, rows, width), BF16),
            shape((2, rows, width), BF16),
        ],
        (
            mine, from_left, from_right, across,
            o_weight, prob, queries[0], held, near, far, context[0],
        ),
        [WHOLE] * 4 + [RAW] + [WHOLE] * 6,
        2 * rows * features * tensors * width + 8 * rows * window * width,
        2 * features * tensors * width,
        [
            pltpu.VMEM((rows, width), BF16),
            pltpu.VMEM(o_weight.shape[1:], BF16),
            pltpu.SemaphoreType.DMA((4,)),
        ],
    )
    near_back = shifted(near_part, -1)
    far_back = shifted(far_part, -2)
    sums = (own_part + near_back.astype(F32) + far_back.astype(F32)).astype(BF16)

    weight_grad, *terms = call(
        weight_kernel,
        [shape((lanes, width), F32)] + [shape((lanes, width), BF16)] * (owners - 1),
        (columns_all, *blocks),
        [WHOLE] * (1 + chips),
        2 * columns_all.size * width,
        2 * (columns_all.size + chips * context.size),
    )
    for mask in range(1, owners):
        other = swapped(terms[mask - 1], mask)
        weight_grad = weight_grad + other.astype(F32)
    return query_grad[None], sums[:1], sums[1:], weight_grad[None]


def solution(mesh):
    sections, shards, tensors = mesh.devices.shape
    split = Mesh(
        mesh.devices.reshape(sections, shards // (CORES * NEAR), NEAR, CORES, tensors),
        ("section", *DP, "tensor"),
    )
    placed = P("section", DP, "tensor")

    return jax.shard_map(
        on_device,
        mesh=split,
        in_specs=(
            P(DP, "tensor"), placed, placed, placed, placed, placed,
            P("section", None, "tensor"), P(),
        ),
        out_specs=(placed,) * 4,
        check_vma=False,
    )
```

```python
import functools

import jax
import jax.numpy as jnp
from jax import lax
from jax.experimental import pallas as pl
from jax.experimental.pallas import tpu as pltpu
from jax.sharding import Mesh, PartitionSpec as P


HD = 128
REACH = 2
CORES = 2
NEAR = 2
F32 = jnp.float32
BF16 = jnp.bfloat16
WHOLE = pl.BlockSpec(memory_space=pltpu.VMEM)
RAW = pl.BlockSpec(memory_space=pltpu.HBM)
DP = ("zh", "zl", "core")
GROUP = ("zl", "core")


def contract(a, b, left, right):
    return lax.dot_general(
        a, b, (((left,), (right,)), ((), ())), preferred_element_type=F32
    )


def shifted(value, steps):
    count = lax.axis_size(DP)
    return lax.ppermute(value, DP, [(i, (i + steps) % count) for i in range(count)])


def turned(value, axis, steps):
    count = lax.axis_size(axis)
    return lax.ppermute(value, axis, [(i, (i + steps) % count) for i in range(count)])


def swapped(value, mask):
    count = lax.axis_size(GROUP)
    return lax.ppermute(value, GROUP, [(i, i ^ mask) for i in range(count)])


def exchanged(value, axis):
    return lax.all_to_all(value, axis, 0, 0, tiled=True)


def spread(value, axis):
    copies = lax.axis_size(axis)
    return exchanged(jnp.broadcast_to(value[None], (copies, *value.shape)), axis)


def copy_all(copies):
    for copy in copies:
        copy.start()
    for copy in copies:
        copy.wait()


def pack_kernel(keys_ref, values_ref, out_grad_ref, held_ref, base_ref, sems):
    rows = base_ref.shape[0]
    at = pl.multiple_of(lax.axis_index("section") * rows, rows)
    copy_all(
        [
            pltpu.make_async_copy(keys_ref.at[0], held_ref.at[0], sems.at[0]),
            pltpu.make_async_copy(values_ref.at[0], held_ref.at[1], sems.at[1]),
            pltpu.make_async_copy(out_grad_ref.at[pl.ds(at, rows), :], base_ref, sems.at[2]),
        ]
    )


def suffix_kernel(base_ref, layers_ref, grads_ref):
    base = base_ref[...].astype(F32)
    upper = None
    for layer in range(layers_ref.shape[0] - 1, -1, -1):
        own = layers_ref[layer].astype(F32)
        upper = own if upper is None else upper + own
        grads = (base + 0.25 * upper).astype(BF16)
        for copy in range(grads_ref.shape[0]):
            grads_ref[copy, layer] = grads


def quarter_kernel(grad_ref, mine_ref):
    blocks, rows, lanes = mine_ref.shape
    each = blocks // grad_ref.shape[0]
    at = pl.multiple_of(lax.axis_index("tensor") * rows, rows)
    for block in range(blocks):
        first = block % each * lanes
        mine_ref[block] = grad_ref[block // each, pl.ds(at, rows), first : first + lanes]


def prob_kernel(
    lengths_hbm, query_hbm, own_ref, near_ref, far_ref,
    prob_ref, lengths_ref, query_ref, sems,
):
    lengths_copy = pltpu.make_async_copy(lengths_hbm, lengths_ref, sems.at[0])
    query_copy = pltpu.make_async_copy(query_hbm.at[0], query_ref, sems.at[1])
    lengths_copy.start()
    query_copy.start()
    rows, width = query_ref.shape
    window = (REACH + 1) * rows
    block = lax.axis_index(DP)
    first = block * rows
    place = first + lax.broadcasted_iota(jnp.int32, (rows, window), 0)
    keys = first - REACH * rows + lax.broadcasted_iota(jnp.int32, (rows, window), 1)
    narrow = first + lax.broadcasted_iota(jnp.int32, (rows, HD), 0)

    def advance(k, carry):
        end, start = carry
        end = end + lengths_ref[k]
        return end, jnp.where(narrow >= end, end, start)

    lengths_copy.wait()
    start = lax.fori_loop(
        0, lengths_ref.shape[0], advance, (jnp.int32(0), jnp.zeros((rows, HD), jnp.int32))
    )[1]
    start = jnp.concatenate([start] * (window // HD), axis=1)
    allowed = (keys <= place) & (keys >= start)
    query_copy.wait()
    for head in range(width // HD):
        cols = slice(head * HD, (head + 1) * HD)
        query = query_ref[:, cols]
        scores = jnp.concatenate(
            [contract(query, ref[0, :, cols], 1, 1) for ref in (far_ref, near_ref, own_ref)],
            axis=1,
        )
        scores = jnp.where(allowed, scores * HD ** (-0.5), -jnp.inf)
        top = jnp.max(scores, axis=-1, keepdims=True)
        weight = jnp.exp(scores - top)
        prob_ref[head] = weight / jnp.sum(weight, axis=-1, keepdims=True)


def grads_kernel(
    grad_ref, weight_hbm, prob_ref, query_ref, own_ref, near_ref, far_ref, context_ref,
    query_grad_ref, own_part_ref, near_part_ref, far_part_ref,
    weight_ref, sems,
):
    parts, rows, depth = grad_ref.shape
    copies = [
        pltpu.make_async_copy(
            weight_hbm.at[0, pl.ds(part * depth, depth)],
            weight_ref.at[pl.ds(part * depth, depth)],
            sems.at[part],
        )
        for part in range(parts)
    ]
    for copy in copies:
        copy.start()
    total = None
    for part in range(parts):
        copies[part].wait()
        term = jnp.dot(
            grad_ref[part],
            weight_ref[part * depth : (part + 1) * depth, :],
            preferred_element_type=F32,
        )
        total = term if total is None else total + term
    d_context = total.astype(BF16)
    blocks = ((far_ref, far_part_ref), (near_ref, near_part_ref), (own_ref, own_part_ref))
    for head in range(query_ref.shape[1] // HD):
        cols = slice(head * HD, (head + 1) * HD)
        query = query_ref[:, cols]
        dctx = d_context[:, cols]
        delta = jnp.sum(
            dctx.astype(F32) * context_ref[:, cols].astype(F32), axis=-1, keepdims=True
        )
        query_grad = None
        for index, (held, part_ref) in enumerate(blocks):
            prob = prob_ref[head, :, index * rows : (index + 1) * rows]
            d_prob = contract(dctx, held[1, :, cols], 1, 1)
            d_score = (prob * (d_prob - delta) * HD ** (-0.5)).astype(BF16)
            term = jnp.dot(d_score, held[0, :, cols], preferred_element_type=F32)
            query_grad = term if query_grad is None else query_grad + term
            part_ref[0, :, cols] = contract(d_score, query, 0, 0).astype(part_ref.dtype)
            part_ref[1, :, cols] = contract(prob.astype(BF16), dctx, 0, 0).astype(part_ref.dtype)
        query_grad_ref[:, cols] = query_grad.astype(BF16)


def weight_kernel(masks, grad_ref, *refs):
    quarters, blocks, _, rows, _ = grad_ref.shape
    context_refs, term_refs = refs[:blocks], refs[blocks:]
    here, me = lax.axis_index("zh"), lax.axis_index(GROUP)
    places = [lax.rem(here + steps, blocks) for steps in ring_steps(blocks)]
    contexts = [
        jnp.concatenate([ref[quarter * rows : (quarter + 1) * rows] for ref in context_refs], axis=0)
        for quarter in range(quarters)
    ]
    for mask, term_ref in zip(masks, term_refs):
        owner = jnp.bitwise_xor(me, mask)
        total = None
        for quarter in range(quarters):
            grad = jnp.concatenate([grad_ref[quarter, at, owner] for at in places], axis=0)
            term = contract(grad, contexts[quarter], 0, 0)
            total = term if total is None else total + term
        term_ref[...] = total.astype(term_ref.dtype)


def ring_steps(count):
    steps = [0]
    for hop in range(1, count // 2 + 1):
        steps.append(count - hop)
        if hop < count - hop:
            steps.append(hop)
    return steps


def call(kernel, outs, inputs, specs, flops, nbytes, scratch=()):
    return pl.pallas_call(
        kernel,
        out_shape=outs,
        in_specs=specs,
        out_specs=[WHOLE] * len(outs),
        scratch_shapes=list(scratch),
        compiler_params=pltpu.CompilerParams(vmem_limit_bytes=24 * 2**20),
        cost_estimate=pl.CostEstimate(flops=flops, bytes_accessed=nbytes, transcendentals=0),
    )(
        *(
            pltpu.with_memory_space_constraint(value, pltpu.HBM) if spec is RAW else value
            for value, spec in zip(inputs, specs)
        )
    )


def on_device(out_grad, section_out, context, queries, key_heads, values, o_weight, doc_lengths):
    rows, width = queries.shape[1:]
    features = out_grad.shape[1]
    sections, tensors, chips = (lax.axis_size(a) for a in ("section", "tensor", "zh"))
    owners = lax.axis_size(GROUP)
    heads = width // HD
    window = (REACH + 1) * rows
    quarter = rows // tensors
    lanes = features * tensors // (chips * owners)
    slab = (sections, rows // sections, features)
    shape = jax.ShapeDtypeStruct

    layers = exchanged(section_out.reshape(slab), "section")
    held, base = call(
        pack_kernel,
        [shape((2, rows, width), BF16), shape(slab[1:], BF16)],
        (key_heads, values, out_grad),
        [RAW] * 3,
        0,
        8 * rows * width,
        [pltpu.SemaphoreType.DMA((3,))],
    )
    blocks = [context[0]]
    for hop in range(1, chips // 2 + 1):
        blocks.append(turned(blocks[max(len(blocks) - 2, 0)], "zh", 1))
        if hop < chips - hop:
            blocks.append(turned(blocks[max(len(blocks) - 2, 0)], "zh", -1))
    near = shifted(held, 1)
    far = shifted(held, 2)
    (grads,) = call(
        suffix_kernel,
        [shape((tensors, *slab), BF16)],
        (base, layers),
        [WHOLE] * 2,
        layers.size * 3,
        layers.size * 4,
    )
    grad_full = exchanged(
        grads.reshape(tensors * sections, *slab[1:]), ("tensor", "section")
    ).reshape(tensors, rows, features)
    (prob,) = call(
        prob_kernel,
        [shape((heads, rows, window), F32)],
        (doc_lengths, queries, held, near, far),
        [RAW] * 2 + [WHOLE] * 3,
        heads * rows * window * (2 * HD + 10),
        heads * rows * window * 8,
        [
            pltpu.SMEM(doc_lengths.shape, jnp.int32),
            pltpu.VMEM((rows, width), BF16),
            pltpu.SemaphoreType.DMA((2,)),
        ],
    )
    (mine,) = call(
        quarter_kernel,
        [shape((chips * owners, quarter, lanes), BF16)],
        (grad_full,),
        [WHOLE],
        0,
        4 * rows * features,
    )
    columns = exchanged(mine.reshape(chips, owners, quarter, lanes), "zh")
    columns_all = spread(columns, "tensor")

    query_grad, own_part, near_part, far_part = call(
        grads_kernel,
        [
            shape((rows, width), BF16),
            shape((2, rows, width), F32),
            shape((2, rows, width), BF16),
            shape((2, rows, width), BF16),
        ],
        (grad_full, o_weight, prob, queries[0], held, near, far, context[0]),
        [WHOLE, RAW] + [WHOLE] * 6,
        2 * rows * features * tensors * width + 8 * rows * window * width,
        2 * features * tensors * width,
        [
            pltpu.VMEM(o_weight.shape[1:], BF16),
            pltpu.SemaphoreType.DMA((tensors,)),
        ],
    )
    near_back = shifted(near_part, -1)
    far_back = shifted(far_part, -2)
    sums = (own_part + near_back.astype(F32) + far_back.astype(F32)).astype(BF16)

    def terms_for(masks, types):
        return call(
            functools.partial(weight_kernel, masks),
            [shape((lanes, width), dtype) for dtype in types],
            (columns_all, *blocks),
            [WHOLE] * (1 + chips),
            len(masks) * columns_all.size * width // 2,
            2 * (columns_all.size + chips * context.size),
        )

    sent = range(owners - 1, 0, -1)
    far_terms = terms_for(sent[:2], [BF16] * 2)
    *near_terms, weight_grad = terms_for((*sent[2:], 0), [BF16] * len(sent[2:]) + [F32])
    for mask, term in zip(sent, (*far_terms, *near_terms)):
        other = swapped(term, mask)
        weight_grad = weight_grad + other.astype(F32)
    return query_grad[None], sums[:1], sums[1:], weight_grad[None]


def solution(mesh):
    sections, shards, tensors = mesh.devices.shape
    split = Mesh(
        mesh.devices.reshape(sections, shards // (CORES * NEAR), NEAR, CORES, tensors),
        ("section", *DP, "tensor"),
    )
    placed = P("section", DP, "tensor")

    return jax.shard_map(
        on_device,
        mesh=split,
        in_specs=(
            P(DP, "tensor"), placed, placed, placed, placed, placed,
            P("section", None, "tensor"), P(),
        ),
        out_specs=(placed,) * 4,
        check_vma=False,
    )
```

```python
import functools

import jax
import jax.numpy as jnp
from jax import lax
from jax.experimental import pallas as pl
from jax.experimental.pallas import tpu as pltpu
from jax.sharding import Mesh, PartitionSpec as P


HD = 128
REACH = 2
CORES = 2
NEAR = 2
F32 = jnp.float32
BF16 = jnp.bfloat16
WHOLE = pl.BlockSpec(memory_space=pltpu.VMEM)
RAW = pl.BlockSpec(memory_space=pltpu.HBM)
DP = ("zh", "zl", "core")
GROUP = ("zl", "core")


def contract(a, b, left, right):
    return lax.dot_general(
        a, b, (((left,), (right,)), ((), ())), preferred_element_type=F32
    )


def shifted(value, steps):
    count = lax.axis_size(DP)
    return lax.ppermute(value, DP, [(i, (i + steps) % count) for i in range(count)])


def turned(value, axis, steps):
    count = lax.axis_size(axis)
    return lax.ppermute(value, axis, [(i, (i + steps) % count) for i in range(count)])


def swapped(value, mask):
    count = lax.axis_size(GROUP)
    return lax.ppermute(value, GROUP, [(i, i ^ mask) for i in range(count)])


def exchanged(value, axis):
    return lax.all_to_all(value, axis, 0, 0, tiled=True)


def copy_all(copies):
    for copy in copies:
        copy.start()
    for copy in copies:
        copy.wait()


def pack_kernel(keys_ref, values_ref, out_grad_ref, held_ref, base_ref, sems):
    rows = base_ref.shape[0]
    at = pl.multiple_of(lax.axis_index("section") * rows, rows)
    copy_all(
        [
            pltpu.make_async_copy(keys_ref.at[0], held_ref.at[0], sems.at[0]),
            pltpu.make_async_copy(values_ref.at[0], held_ref.at[1], sems.at[1]),
            pltpu.make_async_copy(out_grad_ref.at[pl.ds(at, rows), :], base_ref, sems.at[2]),
        ]
    )


def suffix_kernel(base_ref, layers_ref, grads_ref):
    base = base_ref[...].astype(F32)
    upper = None
    for layer in range(layers_ref.shape[0] - 1, -1, -1):
        own = layers_ref[layer].astype(F32)
        upper = own if upper is None else upper + own
        grads = (base + 0.25 * upper).astype(BF16)
        for copy in range(grads_ref.shape[0]):
            grads_ref[copy, layer] = grads


def quarter_kernel(grad_ref, mine_ref):
    blocks, rows, lanes = mine_ref.shape
    each = blocks // grad_ref.shape[0]
    at = pl.multiple_of(lax.axis_index("tensor") * rows, rows)
    for block in range(blocks):
        first = block % each * lanes
        mine_ref[block] = grad_ref[block // each, pl.ds(at, rows), first : first + lanes]


def repeat_kernel(value_ref, repeated_ref, held_ref, sems):
    copy_all([pltpu.make_async_copy(value_ref, held_ref, sems.at[0])])
    copy_all(
        [
            pltpu.make_async_copy(held_ref, repeated_ref.at[at], sems.at[1 + at])
            for at in range(repeated_ref.shape[0])
        ]
    )


def prob_kernel(
    lengths_hbm, query_hbm, own_ref, near_ref, far_ref,
    prob_ref, lengths_ref, query_ref, sems,
):
    lengths_copy = pltpu.make_async_copy(lengths_hbm, lengths_ref, sems.at[0])
    query_copy = pltpu.make_async_copy(query_hbm.at[0], query_ref, sems.at[1])
    lengths_copy.start()
    query_copy.start()
    rows, width = query_ref.shape
    window = (REACH + 1) * rows
    block = lax.axis_index(DP)
    first = block * rows
    place = first + lax.broadcasted_iota(jnp.int32, (rows, window), 0)
    keys = first - REACH * rows + lax.broadcasted_iota(jnp.int32, (rows, window), 1)
    narrow = first + lax.broadcasted_iota(jnp.int32, (rows, HD), 0)

    def advance(k, carry):
        end, start = carry
        end = end + lengths_ref[k]
        return end, jnp.where(narrow >= end, end, start)

    lengths_copy.wait()
    start = lax.fori_loop(
        0, lengths_ref.shape[0], advance, (jnp.int32(0), jnp.zeros((rows, HD), jnp.int32))
    )[1]
    start = jnp.concatenate([start] * (window // HD), axis=1)
    allowed = (keys <= place) & (keys >= start)
    query_copy.wait()
    for head in range(width // HD):
        cols = slice(head * HD, (head + 1) * HD)
        query = query_ref[:, cols]
        scores = jnp.concatenate(
            [contract(query, ref[0, :, cols], 1, 1) for ref in (far_ref, near_ref, own_ref)],
            axis=1,
        )
        scores = jnp.where(allowed, scores * HD ** (-0.5), -jnp.inf)
        top = jnp.max(scores, axis=-1, keepdims=True)
        weight = jnp.exp(scores - top)
        prob_ref[head] = weight / jnp.sum(weight, axis=-1, keepdims=True)


def grads_kernel(
    grad_ref, weight_hbm, prob_ref, query_ref, own_ref, near_ref, far_ref, context_ref,
    query_grad_ref, own_part_ref, near_part_ref, far_part_ref,
    weight_ref, sems,
):
    parts, rows, depth = grad_ref.shape
    copies = [
        pltpu.make_async_copy(
            weight_hbm.at[0, pl.ds(part * depth, depth)],
            weight_ref.at[pl.ds(part * depth, depth)],
            sems.at[part],
        )
        for part in range(parts)
    ]
    for copy in copies:
        copy.start()
    total = None
    for part in range(parts):
        copies[part].wait()
        term = jnp.dot(
            grad_ref[part],
            weight_ref[part * depth : (part + 1) * depth, :],
            preferred_element_type=F32,
        )
        total = term if total is None else total + term
    d_context = total.astype(BF16)
    blocks = ((far_ref, far_part_ref), (near_ref, near_part_ref), (own_ref, own_part_ref))
    for head in range(query_ref.shape[1] // HD):
        cols = slice(head * HD, (head + 1) * HD)
        query = query_ref[:, cols]
        dctx = d_context[:, cols]
        delta = jnp.sum(
            dctx.astype(F32) * context_ref[:, cols].astype(F32), axis=-1, keepdims=True
        )
        query_grad = None
        for index, (held, part_ref) in enumerate(blocks):
            prob = prob_ref[head, :, index * rows : (index + 1) * rows]
            d_prob = contract(dctx, held[1, :, cols], 1, 1)
            d_score = (prob * (d_prob - delta) * HD ** (-0.5)).astype(BF16)
            term = jnp.dot(d_score, held[0, :, cols], preferred_element_type=F32)
            query_grad = term if query_grad is None else query_grad + term
            part_ref[0, :, cols] = contract(d_score, query, 0, 0).astype(part_ref.dtype)
            part_ref[1, :, cols] = contract(prob.astype(BF16), dctx, 0, 0).astype(part_ref.dtype)
        query_grad_ref[:, cols] = query_grad.astype(BF16)


def weight_kernel(masks, grad_ref, *refs):
    quarters, blocks, _, rows, _ = grad_ref.shape
    context_refs, term_refs = refs[:blocks], refs[blocks:]
    here, me = lax.axis_index("zh"), lax.axis_index(GROUP)
    places = [lax.rem(here + steps, blocks) for steps in ring_steps(blocks)]
    contexts = [
        jnp.concatenate([ref[quarter * rows : (quarter + 1) * rows] for ref in context_refs], axis=0)
        for quarter in range(quarters)
    ]
    for mask, term_ref in zip(masks, term_refs):
        owner = jnp.bitwise_xor(me, mask)
        total = None
        for quarter in range(quarters):
            grad = jnp.concatenate([grad_ref[quarter, at, owner] for at in places], axis=0)
            term = contract(grad, contexts[quarter], 0, 0)
            total = term if total is None else total + term
        term_ref[...] = total.astype(term_ref.dtype)


def ring_steps(count):
    steps = [0]
    for hop in range(1, count // 2 + 1):
        steps.append(count - hop)
        if hop < count - hop:
            steps.append(hop)
    return steps


def call(kernel, outs, inputs, specs, flops, nbytes, scratch=(), out_spec=WHOLE):
    return pl.pallas_call(
        kernel,
        out_shape=outs,
        in_specs=specs,
        out_specs=[out_spec] * len(outs),
        scratch_shapes=list(scratch),
        compiler_params=pltpu.CompilerParams(vmem_limit_bytes=24 * 2**20),
        cost_estimate=pl.CostEstimate(flops=flops, bytes_accessed=nbytes, transcendentals=0),
    )(
        *(
            pltpu.with_memory_space_constraint(value, pltpu.HBM) if spec is RAW else value
            for value, spec in zip(inputs, specs)
        )
    )


def on_device(out_grad, section_out, context, queries, key_heads, values, o_weight, doc_lengths):
    rows, width = queries.shape[1:]
    features = out_grad.shape[1]
    sections, tensors, chips = (lax.axis_size(a) for a in ("section", "tensor", "zh"))
    owners = lax.axis_size(GROUP)
    heads = width // HD
    window = (REACH + 1) * rows
    quarter = rows // tensors
    lanes = features * tensors // (chips * owners)
    slab = (sections, rows // sections, features)
    shape = jax.ShapeDtypeStruct

    layers = exchanged(section_out.reshape(slab), "section")
    held, base = call(
        pack_kernel,
        [shape((2, rows, width), BF16), shape(slab[1:], BF16)],
        (key_heads, values, out_grad),
        [RAW] * 3,
        0,
        8 * rows * width,
        [pltpu.SemaphoreType.DMA((3,))],
    )
    blocks = [context[0]]
    for hop in range(1, chips // 2 + 1):
        blocks.append(turned(blocks[max(len(blocks) - 2, 0)], "zh", 1))
        if hop < chips - hop:
            blocks.append(turned(blocks[max(len(blocks) - 2, 0)], "zh", -1))
    near = shifted(held, 1)
    far = shifted(held, 2)
    (grads,) = call(
        suffix_kernel,
        [shape((tensors, *slab), BF16)],
        (base, layers),
        [WHOLE] * 2,
        layers.size * 3,
        layers.size * 4,
    )
    grad_full = exchanged(
        grads.reshape(tensors * sections, *slab[1:]), ("tensor", "section")
    ).reshape(tensors, rows, features)
    (prob,) = call(
        prob_kernel,
        [shape((heads, rows, window), F32)],
        (doc_lengths, queries, held, near, far),
        [RAW] * 2 + [WHOLE] * 3,
        heads * rows * window * (2 * HD + 10),
        heads * rows * window * 8,
        [
            pltpu.SMEM(doc_lengths.shape, jnp.int32),
            pltpu.VMEM((rows, width), BF16),
            pltpu.SemaphoreType.DMA((2,)),
        ],
    )
    (mine,) = call(
        quarter_kernel,
        [shape((chips * owners, quarter, lanes), BF16)],
        (grad_full,),
        [WHOLE],
        0,
        4 * rows * features,
    )
    columns = exchanged(mine.reshape(chips, owners, quarter, lanes), "zh")
    (repeated,) = call(
        repeat_kernel,
        [shape((tensors, *columns.shape), BF16)],
        (columns,),
        [RAW],
        0,
        2 * (tensors + 1) * columns.size,
        [pltpu.VMEM(columns.shape, BF16), pltpu.SemaphoreType.DMA((1 + tensors,))],
        RAW,
    )
    columns_all = exchanged(repeated, "tensor")

    query_grad, own_part, near_part, far_part = call(
        grads_kernel,
        [
            shape((rows, width), BF16),
            shape((2, rows, width), F32),
            shape((2, rows, width), BF16),
            shape((2, rows, width), BF16),
        ],
        (grad_full, o_weight, prob, queries[0], held, near, far, context[0]),
        [WHOLE, RAW] + [WHOLE] * 6,
        2 * rows * features * tensors * width + 8 * rows * window * width,
        2 * features * tensors * width,
        [
            pltpu.VMEM(o_weight.shape[1:], BF16),
            pltpu.SemaphoreType.DMA((tensors,)),
        ],
    )
    near_back = shifted(near_part, -1)
    far_back = shifted(far_part, -2)
    sums = (own_part + near_back.astype(F32) + far_back.astype(F32)).astype(BF16)

    def terms_for(masks, types):
        return call(
            functools.partial(weight_kernel, masks),
            [shape((lanes, width), dtype) for dtype in types],
            (columns_all, *blocks),
            [WHOLE] * (1 + chips),
            len(masks) * columns_all.size * width // 2,
            2 * (columns_all.size + chips * context.size),
        )

    sent = range(owners - 1, 0, -1)
    *sent_terms, weight_grad = terms_for((*sent, 0), [BF16] * len(sent) + [F32])
    for mask, term in zip(sent, sent_terms):
        other = swapped(term, mask)
        weight_grad = weight_grad + other.astype(F32)
    return query_grad[None], sums[:1], sums[1:], weight_grad[None]


def solution(mesh):
    sections, shards, tensors = mesh.devices.shape
    split = Mesh(
        mesh.devices.reshape(sections, shards // (CORES * NEAR), NEAR, CORES, tensors),
        ("section", *DP, "tensor"),
    )
    placed = P("section", DP, "tensor")

    return jax.shard_map(
        on_device,
        mesh=split,
        in_specs=(
            P(DP, "tensor"), placed, placed, placed, placed, placed,
            P("section", None, "tensor"), P(),
        ),
        out_specs=(placed,) * 4,
        check_vma=False,
    )
```

```python
import functools

import jax
import jax.numpy as jnp
from jax import lax
from jax.experimental import pallas as pl
from jax.experimental.pallas import tpu as pltpu
from jax.sharding import Mesh, PartitionSpec as P


HD = 128
REACH = 2
CORES = 2
NEAR = 2
F32 = jnp.float32
BF16 = jnp.bfloat16
WHOLE = pl.BlockSpec(memory_space=pltpu.VMEM)
RAW = pl.BlockSpec(memory_space=pltpu.HBM)
DP = ("zh", "zl", "core")
GROUP = ("zl", "core")


def contract(a, b, left, right):
    return lax.dot_general(
        a, b, (((left,), (right,)), ((), ())), preferred_element_type=F32
    )


def shifted(value, steps):
    count = lax.axis_size(DP)
    return lax.ppermute(value, DP, [(i, (i + steps) % count) for i in range(count)])


def turned(value, axis, steps):
    count = lax.axis_size(axis)
    return lax.ppermute(value, axis, [(i, (i + steps) % count) for i in range(count)])


def swapped(value, mask):
    count = lax.axis_size(GROUP)
    return lax.ppermute(value, GROUP, [(i, i ^ mask) for i in range(count)])


def exchanged(value, axis):
    return lax.all_to_all(value, axis, 0, 0, tiled=True)


def copy_all(copies):
    for copy in copies:
        copy.start()
    for copy in copies:
        copy.wait()


def pack_kernel(keys_ref, values_ref, out_grad_ref, held_ref, base_ref, sems):
    rows = base_ref.shape[0]
    at = pl.multiple_of(lax.axis_index("section") * rows, rows)
    copy_all(
        [
            pltpu.make_async_copy(keys_ref.at[0], held_ref.at[0], sems.at[0]),
            pltpu.make_async_copy(values_ref.at[0], held_ref.at[1], sems.at[1]),
            pltpu.make_async_copy(out_grad_ref.at[pl.ds(at, rows), :], base_ref, sems.at[2]),
        ]
    )


def suffix_kernel(base_ref, layers_ref, grads_ref):
    base = base_ref[...].astype(F32)
    upper = None
    for layer in range(layers_ref.shape[0] - 1, -1, -1):
        own = layers_ref[layer].astype(F32)
        upper = own if upper is None else upper + own
        grads = (base + 0.25 * upper).astype(BF16)
        for copy in range(grads_ref.shape[1]):
            grads_ref[layer, copy] = grads


def quarter_kernel(grad_ref, mine_ref):
    _, tensors, slab_rows, _ = grad_ref.shape
    blocks, rows, lanes = mine_ref.shape
    each = blocks // tensors
    slabs = rows // slab_rows
    at = lax.axis_index("tensor") * slabs
    for block in range(blocks):
        first = block % each * lanes
        for slab in range(slabs):
            mine_ref[block, slab * slab_rows : (slab + 1) * slab_rows] = grad_ref[
                at + slab, block // each, :, first : first + lanes
            ]


def repeat_kernel(value_ref, repeated_ref, held_ref, sems):
    copy_all([pltpu.make_async_copy(value_ref, held_ref, sems.at[0])])
    copy_all(
        [
            pltpu.make_async_copy(held_ref, repeated_ref.at[at], sems.at[1 + at])
            for at in range(repeated_ref.shape[0])
        ]
    )


def prob_kernel(
    lengths_hbm, query_hbm, own_ref, near_ref, far_ref,
    prob_ref, lengths_ref, query_ref, sems,
):
    lengths_copy = pltpu.make_async_copy(lengths_hbm, lengths_ref, sems.at[0])
    query_copy = pltpu.make_async_copy(query_hbm.at[0], query_ref, sems.at[1])
    lengths_copy.start()
    query_copy.start()
    rows, width = query_ref.shape
    window = (REACH + 1) * rows
    block = lax.axis_index(DP)
    first = block * rows
    place = first + lax.broadcasted_iota(jnp.int32, (rows, window), 0)
    keys = first - REACH * rows + lax.broadcasted_iota(jnp.int32, (rows, window), 1)
    narrow = first + lax.broadcasted_iota(jnp.int32, (rows, HD), 0)

    def advance(k, carry):
        end, start = carry
        end = end + lengths_ref[k]
        return end, jnp.where(narrow >= end, end, start)

    lengths_copy.wait()
    start = lax.fori_loop(
        0, lengths_ref.shape[0], advance, (jnp.int32(0), jnp.zeros((rows, HD), jnp.int32))
    )[1]
    start = jnp.concatenate([start] * (window // HD), axis=1)
    allowed = (keys <= place) & (keys >= start)
    query_copy.wait()
    for head in range(width // HD):
        cols = slice(head * HD, (head + 1) * HD)
        query = query_ref[:, cols]
        scores = jnp.concatenate(
            [contract(query, ref[0, :, cols], 1, 1) for ref in (far_ref, near_ref, own_ref)],
            axis=1,
        )
        scores = jnp.where(allowed, scores * HD ** (-0.5), -jnp.inf)
        top = jnp.max(scores, axis=-1, keepdims=True)
        weight = jnp.exp(scores - top)
        prob_ref[head] = weight / jnp.sum(weight, axis=-1, keepdims=True)


def grads_kernel(
    grad_ref, weight_hbm, prob_ref, query_ref, own_ref, near_ref, far_ref, context_ref,
    query_grad_ref, own_part_ref, near_part_ref, far_part_ref,
    weight_ref, sems,
):
    slabs, parts, _, depth = grad_ref.shape
    rows = query_ref.shape[0]
    copies = [
        pltpu.make_async_copy(
            weight_hbm.at[0, pl.ds(part * depth, depth)],
            weight_ref.at[pl.ds(part * depth, depth)],
            sems.at[part],
        )
        for part in range(parts)
    ]
    for copy in copies:
        copy.start()
    total = None
    for part in range(parts):
        copies[part].wait()
        grad = jnp.concatenate([grad_ref[slab, part] for slab in range(slabs)], axis=0)
        term = jnp.dot(
            grad,
            weight_ref[part * depth : (part + 1) * depth, :],
            preferred_element_type=F32,
        )
        total = term if total is None else total + term
    d_context = total.astype(BF16)
    blocks = ((far_ref, far_part_ref), (near_ref, near_part_ref), (own_ref, own_part_ref))
    for head in range(query_ref.shape[1] // HD):
        cols = slice(head * HD, (head + 1) * HD)
        query = query_ref[:, cols]
        dctx = d_context[:, cols]
        delta = jnp.sum(
            dctx.astype(F32) * context_ref[:, cols].astype(F32), axis=-1, keepdims=True
        )
        query_grad = None
        for index, (held, part_ref) in enumerate(blocks):
            prob = prob_ref[head, :, index * rows : (index + 1) * rows]
            d_prob = contract(dctx, held[1, :, cols], 1, 1)
            d_score = (prob * (d_prob - delta) * HD ** (-0.5)).astype(BF16)
            term = jnp.dot(d_score, held[0, :, cols], preferred_element_type=F32)
            query_grad = term if query_grad is None else query_grad + term
            part_ref[0, :, cols] = contract(d_score, query, 0, 0).astype(part_ref.dtype)
            part_ref[1, :, cols] = contract(prob.astype(BF16), dctx, 0, 0).astype(part_ref.dtype)
        query_grad_ref[:, cols] = query_grad.astype(BF16)


def weight_kernel(masks, grad_ref, *refs):
    quarters, blocks, _, rows, _ = grad_ref.shape
    context_refs, term_refs = refs[:blocks], refs[blocks:]
    here, me = lax.axis_index("zh"), lax.axis_index(GROUP)
    places = [lax.rem(here + steps, blocks) for steps in ring_steps(blocks)]
    contexts = [
        jnp.concatenate([ref[quarter * rows : (quarter + 1) * rows] for ref in context_refs], axis=0)
        for quarter in range(quarters)
    ]
    for mask, term_ref in zip(masks, term_refs):
        owner = jnp.bitwise_xor(me, mask)
        total = None
        for quarter in range(quarters):
            grad = jnp.concatenate([grad_ref[quarter, at, owner] for at in places], axis=0)
            term = contract(grad, contexts[quarter], 0, 0)
            total = term if total is None else total + term
        term_ref[...] = total.astype(term_ref.dtype)


def ring_steps(count):
    steps = [0]
    for hop in range(1, count // 2 + 1):
        steps.append(count - hop)
        if hop < count - hop:
            steps.append(hop)
    return steps


def call(kernel, outs, inputs, specs, flops, nbytes, scratch=(), out_spec=WHOLE):
    return pl.pallas_call(
        kernel,
        out_shape=outs,
        in_specs=specs,
        out_specs=[out_spec] * len(outs),
        scratch_shapes=list(scratch),
        compiler_params=pltpu.CompilerParams(vmem_limit_bytes=24 * 2**20),
        cost_estimate=pl.CostEstimate(flops=flops, bytes_accessed=nbytes, transcendentals=0),
    )(
        *(
            pltpu.with_memory_space_constraint(value, pltpu.HBM) if spec is RAW else value
            for value, spec in zip(inputs, specs)
        )
    )


def on_device(out_grad, section_out, context, queries, key_heads, values, o_weight, doc_lengths):
    rows, width = queries.shape[1:]
    features = out_grad.shape[1]
    sections, tensors, chips = (lax.axis_size(a) for a in ("section", "tensor", "zh"))
    owners = lax.axis_size(GROUP)
    heads = width // HD
    window = (REACH + 1) * rows
    quarter = rows // tensors
    lanes = features * tensors // (chips * owners)
    slab = (sections, rows // sections, features)
    shape = jax.ShapeDtypeStruct

    layers = exchanged(section_out.reshape(slab), "section")
    held, base = call(
        pack_kernel,
        [shape((2, rows, width), BF16), shape(slab[1:], BF16)],
        (key_heads, values, out_grad),
        [RAW] * 3,
        0,
        8 * rows * width,
        [pltpu.SemaphoreType.DMA((3,))],
    )
    blocks = [context[0]]
    for hop in range(1, chips // 2 + 1):
        blocks.append(turned(blocks[max(len(blocks) - 2, 0)], "zh", 1))
        if hop < chips - hop:
            blocks.append(turned(blocks[max(len(blocks) - 2, 0)], "zh", -1))
    near = shifted(held, 1)
    far = shifted(held, 2)
    (grads,) = call(
        suffix_kernel,
        [shape((sections, tensors, *slab[1:]), BF16)],
        (base, layers),
        [WHOLE] * 2,
        layers.size * 3,
        layers.size * 4,
    )
    grad_full = exchanged(
        grads.reshape(sections * tensors, *slab[1:]), ("section", "tensor")
    ).reshape(grads.shape)
    (prob,) = call(
        prob_kernel,
        [shape((heads, rows, window), F32)],
        (doc_lengths, queries, held, near, far),
        [RAW] * 2 + [WHOLE] * 3,
        heads * rows * window * (2 * HD + 10),
        heads * rows * window * 8,
        [
            pltpu.SMEM(doc_lengths.shape, jnp.int32),
            pltpu.VMEM((rows, width), BF16),
            pltpu.SemaphoreType.DMA((2,)),
        ],
    )
    (mine,) = call(
        quarter_kernel,
        [shape((chips * owners, quarter, lanes), BF16)],
        (grad_full,),
        [WHOLE],
        0,
        4 * rows * features,
    )
    columns = exchanged(mine.reshape(chips, owners, quarter, lanes), "zh")
    (repeated,) = call(
        repeat_kernel,
        [shape((tensors, *columns.shape), BF16)],
        (columns,),
        [RAW],
        0,
        2 * (tensors + 1) * columns.size,
        [pltpu.VMEM(columns.shape, BF16), pltpu.SemaphoreType.DMA((1 + tensors,))],
        RAW,
    )
    columns_all = exchanged(repeated, "tensor")

    query_grad, own_part, near_part, far_part = call(
        grads_kernel,
        [
            shape((rows, width), BF16),
            shape((2, rows, width), F32),
            shape((2, rows, width), BF16),
            shape((2, rows, width), BF16),
        ],
        (grad_full, o_weight, prob, queries[0], held, near, far, context[0]),
        [WHOLE, RAW] + [WHOLE] * 6,
        2 * rows * features * tensors * width + 8 * rows * window * width,
        2 * features * tensors * width,
        [
            pltpu.VMEM(o_weight.shape[1:], BF16),
            pltpu.SemaphoreType.DMA((tensors,)),
        ],
    )
    near_back = shifted(near_part, -1)
    far_back = shifted(far_part, -2)
    sums = (own_part + near_back.astype(F32) + far_back.astype(F32)).astype(BF16)

    def terms_for(masks, types):
        return call(
            functools.partial(weight_kernel, masks),
            [shape((lanes, width), dtype) for dtype in types],
            (columns_all, *blocks),
            [WHOLE] * (1 + chips),
            len(masks) * columns_all.size * width // 2,
            2 * (columns_all.size + chips * context.size),
        )

    sent = range(owners - 1, 0, -1)
    *sent_terms, weight_grad = terms_for((*sent, 0), [BF16] * len(sent) + [F32])
    for mask, term in zip(sent, sent_terms):
        other = swapped(term, mask)
        weight_grad = weight_grad + other.astype(F32)
    return query_grad[None], sums[:1], sums[1:], weight_grad[None]


def solution(mesh):
    sections, shards, tensors = mesh.devices.shape
    split = Mesh(
        mesh.devices.reshape(sections, shards // (CORES * NEAR), NEAR, CORES, tensors),
        ("section", *DP, "tensor"),
    )
    placed = P("section", DP, "tensor")

    return jax.shard_map(
        on_device,
        mesh=split,
        in_specs=(
            P(DP, "tensor"), placed, placed, placed, placed, placed,
            P("section", None, "tensor"), P(),
        ),
        out_specs=(placed,) * 4,
        check_vma=False,
    )
```

```python
import jax
import jax.numpy as jnp
from jax import lax
from jax.experimental import pallas as pl
from jax.experimental.pallas import tpu as pltpu
from jax.sharding import Mesh, PartitionSpec as P


HD = 128
REACH = 2
CORES = 2
NEAR = 2
F32 = jnp.float32
BF16 = jnp.bfloat16
WHOLE = pl.BlockSpec(memory_space=pltpu.VMEM)
RAW = pl.BlockSpec(memory_space=pltpu.HBM)
DP = ("zh", "zl", "core")
GROUP = ("zl", "core")


def contract(a, b, left, right):
    return lax.dot_general(
        a, b, (((left,), (right,)), ((), ())), preferred_element_type=F32
    )


def shifted(value, steps):
    count = lax.axis_size(DP)
    return lax.ppermute(value, DP, [(i, (i + steps) % count) for i in range(count)])


def turned(value, axis, steps):
    count = lax.axis_size(axis)
    return lax.ppermute(value, axis, [(i, (i + steps) % count) for i in range(count)])


def swapped(value, mask):
    count = lax.axis_size(GROUP)
    return lax.ppermute(value, GROUP, [(i, i ^ mask) for i in range(count)])


def exchanged(value, axis):
    return lax.all_to_all(value, axis, 0, 0, tiled=True)


def spread(value, axis):
    copies = lax.axis_size(axis)
    return exchanged(jnp.broadcast_to(value[None], (copies, *value.shape)), axis)


def copy_all(copies):
    for copy in copies:
        copy.start()
    for copy in copies:
        copy.wait()


def pack_kernel(keys_ref, values_ref, out_grad_ref, held_ref, base_ref, sems):
    rows = base_ref.shape[0]
    at = pl.multiple_of(lax.axis_index("section") * rows, rows)
    copy_all(
        [
            pltpu.make_async_copy(keys_ref.at[0], held_ref.at[0], sems.at[0]),
            pltpu.make_async_copy(values_ref.at[0], held_ref.at[1], sems.at[1]),
            pltpu.make_async_copy(out_grad_ref.at[pl.ds(at, rows), :], base_ref, sems.at[2]),
        ]
    )


def suffix_kernel(base_ref, layers_ref, grads_ref):
    base = base_ref[...].astype(F32)
    upper = None
    for layer in range(layers_ref.shape[0] - 1, -1, -1):
        own = layers_ref[layer].astype(F32)
        upper = own if upper is None else upper + own
        grads_ref[layer] = (base + 0.25 * upper).astype(BF16)


def quarter_kernel(grad_ref, mine_ref):
    blocks, rows, lanes = mine_ref.shape
    each = blocks // grad_ref.shape[0]
    at = pl.multiple_of(lax.axis_index("tensor") * rows, rows)
    for block in range(blocks):
        first = block % each * lanes
        mine_ref[block] = grad_ref[block // each, pl.ds(at, rows), first : first + lanes]


def prob_kernel(
    lengths_hbm, query_hbm, own_ref, near_ref, far_ref,
    prob_ref, lengths_ref, query_ref, sems,
):
    lengths_copy = pltpu.make_async_copy(lengths_hbm, lengths_ref, sems.at[0])
    query_copy = pltpu.make_async_copy(query_hbm.at[0], query_ref, sems.at[1])
    lengths_copy.start()
    query_copy.start()
    rows, width = query_ref.shape
    window = (REACH + 1) * rows
    block = lax.axis_index(DP)
    first = block * rows
    place = first + lax.broadcasted_iota(jnp.int32, (rows, window), 0)
    keys = first - REACH * rows + lax.broadcasted_iota(jnp.int32, (rows, window), 1)
    narrow = first + lax.broadcasted_iota(jnp.int32, (rows, HD), 0)

    def advance(k, carry):
        end, start = carry
        end = end + lengths_ref[k]
        return end, jnp.where(narrow >= end, end, start)

    lengths_copy.wait()
    start = lax.fori_loop(
        0, lengths_ref.shape[0], advance, (jnp.int32(0), jnp.zeros((rows, HD), jnp.int32))
    )[1]
    start = jnp.concatenate([start] * (window // HD), axis=1)
    allowed = (keys <= place) & (keys >= start)
    query_copy.wait()
    for head in range(width // HD):
        cols = slice(head * HD, (head + 1) * HD)
        query = query_ref[:, cols]
        scores = jnp.concatenate(
            [contract(query, ref[0, :, cols], 1, 1) for ref in (far_ref, near_ref, own_ref)],
            axis=1,
        )
        scores = jnp.where(allowed, scores * HD ** (-0.5), -jnp.inf)
        top = jnp.max(scores, axis=-1, keepdims=True)
        weight = jnp.exp(scores - top)
        prob_ref[head] = weight / jnp.sum(weight, axis=-1, keepdims=True)


def grads_kernel(
    grad_ref, weight_hbm, prob_ref, query_ref, own_ref, near_ref, far_ref, context_ref,
    query_grad_ref, own_part_ref, near_part_ref, far_part_ref,
    weight_ref, sems,
):
    parts, rows, depth = grad_ref.shape
    copies = [
        pltpu.make_async_copy(
            weight_hbm.at[0, pl.ds(part * depth, depth)],
            weight_ref.at[pl.ds(part * depth, depth)],
            sems.at[part],
        )
        for part in range(parts)
    ]
    for copy in copies:
        copy.start()
    total = None
    for part in range(parts):
        copies[part].wait()
        term = jnp.dot(
            grad_ref[part],
            weight_ref[part * depth : (part + 1) * depth, :],
            preferred_element_type=F32,
        )
        total = term if total is None else total + term
    d_context = total.astype(BF16)
    blocks = ((far_ref, far_part_ref), (near_ref, near_part_ref), (own_ref, own_part_ref))
    for head in range(query_ref.shape[1] // HD):
        cols = slice(head * HD, (head + 1) * HD)
        query = query_ref[:, cols]
        dctx = d_context[:, cols]
        delta = jnp.sum(
            dctx.astype(F32) * context_ref[:, cols].astype(F32), axis=-1, keepdims=True
        )
        query_grad = None
        for index, (held, part_ref) in enumerate(blocks):
            prob = prob_ref[head, :, index * rows : (index + 1) * rows]
            d_prob = contract(dctx, held[1, :, cols], 1, 1)
            d_score = (prob * (d_prob - delta) * HD ** (-0.5)).astype(BF16)
            term = jnp.dot(d_score, held[0, :, cols], preferred_element_type=F32)
            query_grad = term if query_grad is None else query_grad + term
            part_ref[0, :, cols] = contract(d_score, query, 0, 0).astype(part_ref.dtype)
            part_ref[1, :, cols] = contract(prob.astype(BF16), dctx, 0, 0).astype(part_ref.dtype)
        query_grad_ref[:, cols] = query_grad.astype(BF16)


def weight_kernel(grad_ref, *refs):
    quarters, blocks, owners, rows, _ = grad_ref.shape
    context_refs, term_refs = refs[:blocks], refs[blocks:]
    here, me = lax.axis_index("zh"), lax.axis_index(GROUP)
    places = [lax.rem(here + steps, blocks) for steps in ring_steps(blocks)]
    contexts = [
        jnp.concatenate([ref[quarter * rows : (quarter + 1) * rows] for ref in context_refs], axis=0)
        for quarter in range(quarters)
    ]
    for mask in range(owners):
        owner = jnp.bitwise_xor(me, mask)
        total = None
        for quarter in range(quarters):
            grad = jnp.concatenate([grad_ref[quarter, at, owner] for at in places], axis=0)
            term = contract(grad, contexts[quarter], 0, 0)
            total = term if total is None else total + term
        term_refs[mask][...] = total.astype(term_refs[mask].dtype)


def ring_steps(count):
    steps = [0]
    for hop in range(1, count // 2 + 1):
        steps.append(count - hop)
        if hop < count - hop:
            steps.append(hop)
    return steps


def call(kernel, outs, inputs, specs, flops, nbytes, scratch=()):
    return pl.pallas_call(
        kernel,
        out_shape=outs,
        in_specs=specs,
        out_specs=[WHOLE] * len(outs),
        scratch_shapes=list(scratch),
        compiler_params=pltpu.CompilerParams(vmem_limit_bytes=24 * 2**20),
        cost_estimate=pl.CostEstimate(flops=flops, bytes_accessed=nbytes, transcendentals=0),
    )(
        *(
            pltpu.with_memory_space_constraint(value, pltpu.HBM) if spec is RAW else value
            for value, spec in zip(inputs, specs)
        )
    )


def on_device(out_grad, section_out, context, queries, key_heads, values, o_weight, doc_lengths):
    rows, width = queries.shape[1:]
    features = out_grad.shape[1]
    sections, tensors, chips = (lax.axis_size(a) for a in ("section", "tensor", "zh"))
    owners = lax.axis_size(GROUP)
    heads = width // HD
    window = (REACH + 1) * rows
    quarter = rows // tensors
    lanes = features * tensors // (chips * owners)
    slab = (sections, rows // sections, features)
    shape = jax.ShapeDtypeStruct

    layers = exchanged(section_out.reshape(slab), "section")
    held, base = call(
        pack_kernel,
        [shape((2, rows, width), BF16), shape(slab[1:], BF16)],
        (key_heads, values, out_grad),
        [RAW] * 3,
        0,
        8 * rows * width,
        [pltpu.SemaphoreType.DMA((3,))],
    )
    blocks = [context[0]]
    for hop in range(1, chips // 2 + 1):
        blocks.append(turned(blocks[max(len(blocks) - 2, 0)], "zh", 1))
        if hop < chips - hop:
            blocks.append(turned(blocks[max(len(blocks) - 2, 0)], "zh", -1))
    near = shifted(held, 1)
    far = shifted(held, 2)
    (grads,) = call(
        suffix_kernel,
        [shape(slab, BF16)],
        (base, layers),
        [WHOLE] * 2,
        layers.size * 3,
        layers.size * 4,
    )
    grad_local = exchanged(grads, "section").reshape(rows, features)
    grad_full = spread(grad_local, "tensor")
    (prob,) = call(
        prob_kernel,
        [shape((heads, rows, window), F32)],
        (doc_lengths, queries, held, near, far),
        [RAW] * 2 + [WHOLE] * 3,
        heads * rows * window * (2 * HD + 10),
        heads * rows * window * 8,
        [
            pltpu.SMEM(doc_lengths.shape, jnp.int32),
            pltpu.VMEM((rows, width), BF16),
            pltpu.SemaphoreType.DMA((2,)),
        ],
    )
    (mine,) = call(
        quarter_kernel,
        [shape((chips * owners, quarter, lanes), BF16)],
        (grad_full,),
        [WHOLE],
        0,
        4 * rows * features,
    )
    columns = exchanged(mine.reshape(chips, owners, quarter, lanes), "zh")
    columns_all = spread(columns, "tensor")

    query_grad, own_part, near_part, far_part = call(
        grads_kernel,
        [
            shape((rows, width), BF16),
            shape((2, rows, width), F32),
            shape((2, rows, width), BF16),
            shape((2, rows, width), BF16),
        ],
        (grad_full, o_weight, prob, queries[0], held, near, far, context[0]),
        [WHOLE, RAW] + [WHOLE] * 6,
        2 * rows * features * tensors * width + 8 * rows * window * width,
        2 * features * tensors * width,
        [
            pltpu.VMEM(o_weight.shape[1:], BF16),
            pltpu.SemaphoreType.DMA((tensors,)),
        ],
    )
    near_back = shifted(near_part, -1)
    far_back = shifted(far_part, -2)
    sums = (own_part + near_back.astype(F32) + far_back.astype(F32)).astype(BF16)

    weight_grad, *terms = call(
        weight_kernel,
        [shape((lanes, width), F32)] + [shape((lanes, width), BF16)] * (owners - 1),
        (columns_all, *blocks),
        [WHOLE] * (1 + chips),
        2 * columns_all.size * width,
        2 * (columns_all.size + chips * context.size),
    )
    for mask in range(1, owners):
        other = swapped(terms[mask - 1], mask)
        weight_grad = weight_grad + other.astype(F32)
    return query_grad[None], sums[:1], sums[1:], weight_grad[None]


def solution(mesh):
    sections, shards, tensors = mesh.devices.shape
    split = Mesh(
        mesh.devices.reshape(sections, shards // (CORES * NEAR), NEAR, CORES, tensors),
        ("section", *DP, "tensor"),
    )
    placed = P("section", DP, "tensor")

    return jax.shard_map(
        on_device,
        mesh=split,
        in_specs=(
            P(DP, "tensor"), placed, placed, placed, placed, placed,
            P("section", None, "tensor"), P(),
        ),
        out_specs=(placed,) * 4,
        check_vma=False,
    )
```
